32 devices in a mesh: row: 4 (over z), col: 8 (over y, x, core).
Axes of the slice: x: 2, y: 2, z: 4, core: 2. Of those that a mesh axis runs over, the one named last changes fastest.
Arguments:
- diag_factor: float32 [512, 512], P('row', 'col'), as said below
- panel_factor: float32 [8192, 512], P('row', 'col'), may hold values from -0.0625 to 0.0625
- row_factor: float32 [512, 3072], P('row', 'col'), may hold values from -0.25 to 0.25
- trailing_factor: float32 [8192, 3072], P('row', 'col'), may hold values from -0.0625 to 0.0625
- panel_grad: float32 [8192, 512], P('row', 'col'), may hold values from -6 to 6
- diag_grad: float32 [512, 512], P('row', 'col'), may hold values from -6 to 6
- row_grad: float32 [512, 3072], P('row', 'col'), may hold values from -6 to 6
- trailing_grad: float32 [8192, 3072], P('row', 'col'), may hold values from -6 to 6
Outputs:
- panel_adjoint: float32 [8192, 512], P('row', 'col')
- trailing_out: float32 [8192, 3072], P('row', 'col')
- row_out: float32 [512, 3072], P('row', 'col')
- diag_out: float32 [512, 512], P('row', 'col')
The draws below stay inside these ranges and needn't reach their ends.
Inputs may be any that keep to these rules, and one draw needn't show every extreme that they name: diag_factor is zero above its diagonal; its diagonal entries lie between 1 and 2.
All inputs are finite; a program needn't handle non-finite values.
Results may differ from the reference program's by a relative error of at most 0.00011.
Values sent between devices are 32-bit elements; how exact they have to be, the bound alone decides.
A program may use at most 64 MiB of HBM per device.

```python
import math
import jax
import jax.numpy as jnp
from jax import lax

B = 512
M = 8192
K = 3072


def draw_diag_factor(key, part):
    first = jax.random.fold_in(key, 11)
    second = jax.random.fold_in(key, 23)
    entries = jax.random.normal(first, (B, B), jnp.float32)
    lower = jnp.tril(entries, -1) / math.sqrt(B)
    diagonal = jax.random.uniform(second, (B,), jnp.float32, 1.0, 2.0)
    return lower + jnp.eye(B, dtype=jnp.float32) * diagonal[None, :]


def level_of(key, dims, pieces, least, top_value):
    loudness = 1.0
    for axis_at, parts in pieces:
        heights = jax.random.uniform(jax.random.fold_in(jax.random.fold_in(key, 6), axis_at), (parts,), jnp.float32, least / len(pieces), top_value / len(pieces))
        loudness = loudness * jnp.repeat(jnp.exp(heights), dims[axis_at] // parts).reshape((-1,) + (1,) * (len(dims) - 1 - axis_at))
    return loudness


def noise(rng, shape, width, most, cuts=(), kind=jnp.bfloat16):
    values = jax.random.normal(rng, shape, jnp.float32) * width
    if len(cuts) > 0:
        values = level_of(rng, shape, cuts, -0.22, 0.18) * values
    return jnp.clip(values, min=-most, max=most).astype(kind)


def setup_inputs(seed: int = 0) -> dict:
    seeds = jax.random.split(jax.random.key(seed), 9)
    return {
        "diag_factor": draw_diag_factor(jax.random.fold_in(seeds[8], 71), 0),
        "panel_factor": noise(seeds[1], (M, B), M ** -0.5, 0.0625, ((0, 4), (1, 8)), jnp.float32),
        "row_factor": noise(seeds[2], (B, K), B ** -0.5, 0.25, ((0, 4), (1, 8)), jnp.float32),
        "trailing_factor": noise(seeds[3], (M, K), M ** -0.5, 0.0625, ((0, 4), (1, 8)), jnp.float32),
        "panel_grad": noise(seeds[4], (M, B), 1.0, 6.0, ((0, 4), (1, 8)), jnp.float32),
        "diag_grad": noise(seeds[5], (B, B), 1.0, 6.0, ((0, 4), (1, 8)), jnp.float32),
        "row_grad": noise(seeds[6], (B, K), 1.0, 6.0, ((0, 4), (1, 8)), jnp.float32),
        "trailing_grad": noise(seeds[7], (M, K), 1.0, 6.0, ((0, 4), (1, 8)), jnp.float32),
    }


def reference(diag_factor, panel_factor, row_factor, trailing_factor, panel_grad, diag_grad, row_grad, trailing_grad):
    high = lax.Precision.HIGHEST
    solved = jax.scipy.linalg.solve_triangular(diag_factor, panel_grad.T, lower=True, trans=1).T
    trailing_out = trailing_grad - jnp.dot(solved.astype(jnp.float32), row_factor.astype(jnp.float32), precision=high, preferred_element_type=jnp.float32)
    row_out = row_grad - jnp.dot(solved.T.astype(jnp.float32), trailing_factor.astype(jnp.float32), precision=high, preferred_element_type=jnp.float32)
    block = diag_grad - jnp.dot(solved.T.astype(jnp.float32), panel_factor.astype(jnp.float32), precision=high, preferred_element_type=jnp.float32)
    diag_out = jnp.tril(block)
    return (solved, trailing_out, row_out, diag_out)
```

```python
import functools
import math

import jax
import jax.numpy as jnp
from jax import lax
from jax.experimental import pallas as pl
from jax.experimental.pallas import tpu as pltpu
from jax.sharding import PartitionSpec as P

MESH = pl.DeviceIdType.MESH
F32 = jnp.float32
BF16 = jnp.bfloat16
CORES = 2


def split(x):
    hi = x.astype(BF16)
    return hi, (x - hi.astype(F32)).astype(BF16)


def dot3(a, b, dims=(((1,), (0,)), ((), ()))):
    dot = functools.partial(lax.dot_general, dimension_numbers=dims, preferred_element_type=F32)
    return dot(a[0], b[0]) + (dot(a[0], b[1]) + dot(a[1], b[0]))


def dot_high(a, b):
    return jnp.dot(a, b, precision=lax.Precision.HIGHEST, preferred_element_type=F32)


def iota(shape, dim):
    return lax.broadcasted_iota(jnp.int32, shape, dim)


def invert_base(a):
    n = a.shape[0]
    i, j = iota((n, n), 0), iota((n, n), 1)
    eye = i == j
    d = jnp.where(eye, a, 0.0)
    inv_col = 1.0 / jnp.sum(d, axis=1, keepdims=True)
    inv_row = 1.0 / jnp.sum(d, axis=0, keepdims=True)
    inv = jnp.where(eye, inv_col, 0.0)
    step = 1
    while step < n:
        pair = (i // (2 * step) == j // (2 * step)) & (i // step < j // step)
        part = jnp.where(pair, a, 0.0)
        if step == 1:
            inv = inv - part * inv_col * inv_row
        else:
            inv = inv - dot_high(dot_high(inv, part), inv)
        step *= 2
    return inv


class Gather:
    def __init__(self, place, side, buf, own, sems):
        self.z, self.y, self.x, self.core = place
        self.s, self.buf, self.own = side, buf, own
        self.p1s, self.p1r, self.p2s, self.p2r, self.cs, self.cr = sems

    def col(self, dy, dx, core):
        s = self.s
        return (lax.rem(self.y + dy + s, s) * s + lax.rem(self.x + dx + s, s)) * CORES + core

    def half(self, ref, half):
        rows = self.buf.shape[-2] // 2
        lead = (slice(None),) * (len(ref.shape) - 2)
        return ref.at[lead + (pl.ds(half * rows, rows), slice(None))]

    def block(self, dy, dx, core, half):
        return self.half(self.buf.at[self.col(dy, dx, core)], half)

    def source(self, dy, dx, half):
        if dy == 0 and dx == 0:
            return self.half(self.own, half)
        return self.block(dy, dx, self.core, half)

    def copy(self, dy, dx, half, send, recv, to):
        return pltpu.make_async_remote_copy(
            src_ref=self.source(dy, dx, half),
            dst_ref=self.block(dy, dx, self.core, half),
            send_sem=send,
            recv_sem=recv,
            device_id=(self.z, to),
            device_id_type=MESH,
        )

    def first(self, half, k):
        to = self.col(0, k, self.core) if half == 0 else self.col(k, 0, self.core)
        return self.copy(0, 0, half, self.p1s.at[half, k], self.p1r.at[half, k], to)

    def second(self, half, k, m):
        dy, dx = (0, -k) if half == 0 else (-k, 0)
        to = self.col(m, 0, self.core) if half == 0 else self.col(0, m, self.core)
        return self.copy(dy, dx, half, self.p2s.at[half, k, m], self.p2r.at[half, k, m], to)

    def across(self, dy, dx, half):
        at = dy * self.s + dx
        to = self.col(0, 0, 1 - self.core)
        return self.copy(-dy, -dx, half, self.cs.at[half, at], self.cr.at[half, at], to)

    def start_first(self):
        for k in range(1, self.s):
            for half in range(2):
                self.first(half, k).start()

    def start_own(self):
        for m in range(1, self.s):
            for half in range(2):
                self.second(half, 0, m).start()
        for half in range(2):
            self.across(0, 0, half).start()

    def relay(self):
        for k in range(1, self.s):
            for half in range(2):
                self.first(half, k).wait_recv()
                for m in range(1, self.s):
                    self.second(half, k, m).start()
                dy, dx = (0, k) if half == 0 else (k, 0)
                self.across(dy, dx, half).start()

    def pass_own(self):
        for m in range(1, self.s):
            for half in range(2):
                self.second(half, 0, m).wait_recv()
                dy, dx = (m, 0) if half == 0 else (0, m)
                self.across(dy, dx, half).start()

    def pass_relayed(self):
        for k in range(1, self.s):
            for m in range(1, self.s):
                for half in range(2):
                    self.second(half, k, m).wait_recv()
                    dy, dx = (m, k) if half == 0 else (k, m)
                    self.across(dy, dx, half).start()

    def wait_chip(self, dy, dx):
        for half in range(2):
            self.across(dy, dx, half).wait_recv()

    def wait_sends(self):
        s = self.s
        for half in range(2):
            for k in range(1, s):
                self.first(half, k).wait_send()
            for k in range(s):
                for m in range(1, s):
                    self.second(half, k, m).wait_send()
            for dy in range(s):
                for dx in range(s):
                    self.across(dy, dx, half).wait_send()


def kernel(
    nz, side, dt_hbm, gt_hbm, p_hbm, r_hbm, t_hbm, dg_hbm, rg_hbm, tg_hbm,
    pa_hbm, to_hbm, ro_hbm, do_hbm,
    dbuf, gbuf, rbuf, tbuf, pbuf, dgbuf, rgbuf, tgbuf, pabuf, dobuf,
    aup, inv_t, tp_hi, tp_lo, g_hi, g_lo, wbuf, ubuf, rsbuf,
    d_sems, g_sems, zs, zr, rs_s, rs_r, us, ur, local, outs,
):
    z = lax.axis_index("row")
    c = lax.axis_index("col")
    core = lax.rem(c, CORES)
    chip = c // CORES
    x, y = lax.rem(chip, side), chip // side
    place = (z, y, x, core)
    ncol, w, m = gbuf.shape
    n = ncol * w
    h = n // nz
    k = tbuf.shape[1]
    wide = tp_hi.shape[1]

    dgat = Gather(place, side, dbuf, dbuf.at[c], d_sems)
    ggat = Gather(place, side, gbuf, gt_hbm, g_sems)

    loads = [
        (dt_hbm, dbuf.at[c, z]),
        (t_hbm, tbuf),
        (p_hbm, pbuf),
        (gt_hbm, gbuf.at[c]),
        (r_hbm, rbuf.at[z]),
        (tg_hbm, tgbuf),
        (rg_hbm, rgbuf),
        (dg_hbm, dgbuf),
    ]
    loads = [pltpu.make_async_copy(a, b, local.at[i]) for i, (a, b) in enumerate(loads)]
    for load in loads:
        load.start()

    barrier = pltpu.get_barrier_semaphore()
    peers = [(lax.rem(z + i, nz), c) for i in range(1, nz)]
    peers += [(z, ggat.col(0, i, core)) for i in range(1, side)]
    peers += [(z, ggat.col(i, 0, core)) for i in range(1, side)]
    peers += [(z, ggat.col(0, 0, 1 - core))]
    for peer in peers:
        pl.semaphore_signal(barrier, inc=1, device_id=peer, device_id_type=MESH)
    pl.semaphore_wait(barrier, len(peers))

    def along_z(src, dst, send, recv, i):
        return pltpu.make_async_remote_copy(
            src_ref=src, dst_ref=dst, send_sem=send.at[i], recv_sem=recv.at[i],
            device_id=(lax.rem(z + i, nz), c), device_id_type=MESH,
        )

    d_z = [along_z(dt_hbm, dbuf.at[c, z], zs, zr, i) for i in range(1, nz)]
    r_z = [along_z(r_hbm, rbuf.at[z], rs_s, rs_r, i) for i in range(1, nz)]
    for copy in d_z:
        copy.start()
    ggat.start_first()
    for copy in r_z:
        copy.start()

    loads[0].wait()
    for copy in d_z:
        copy.wait_recv()
    dgat.start_first()
    dgat.start_own()

    for load in loads[1:]:
        load.wait()

    tile = 256

    def widen(i, carry):
        rows = pl.ds(pl.multiple_of(i * tile, tile), tile)
        hi, lo = split(tbuf[rows, :])
        tp_hi[rows, :k] = hi
        tp_lo[rows, :k] = lo
        tail = jnp.concatenate([pbuf[rows, :], jnp.zeros((tile, wide - k - w), F32)], axis=1)
        hi, lo = split(tail)
        tp_hi[rows, k:] = hi
        tp_lo[rows, k:] = lo
        return carry

    dgat.relay()
    ggat.start_own()
    ggat.relay()
    lax.fori_loop(0, m // tile, widen, 0)

    dgat.pass_own()
    dgat.pass_relayed()
    for dy in range(side):
        for dx in range(side):
            dgat.wait_chip(dy, dx)
    for col in range(ncol):
        aup[col * w:(col + 1) * w, :] = jnp.concatenate([dbuf[col, i] for i in range(nz)], axis=1)

    base = 128
    inv_t[...] = jnp.zeros((n, n), F32)
    for b in range(0, n, base):
        inv_t[b:b + base, b:b + base] = invert_base(aup[b:b + base, b:b + base])
    step = base
    while step < n:
        for b in range(0, n, 2 * step):
            up, low = slice(b, b + step), slice(b + step, b + 2 * step)
            inv_t[up, low] = -dot_high(dot_high(inv_t[up, up], aup[up, low]), inv_t[low, low])
        step *= 2

    def take(dy, dx):
        at = ggat.col(-dy, -dx, 0)
        rows = pl.ds(pl.multiple_of(at * w, CORES * w), CORES * w)
        value = split(gbuf[pl.ds(at, CORES)].reshape(CORES * w, m))
        g_hi[rows, :] = value[0]
        g_lo[rows, :] = value[1]
        wbuf[rows, :] = dot3(value, (tp_hi[...], tp_lo[...]))

    ggat.pass_own()
    ggat.wait_chip(0, 0)
    take(0, 0)
    for i in range(1, side):
        ggat.wait_chip(0, i)
        take(0, i)
        ggat.wait_chip(i, 0)
        take(i, 0)
    ggat.pass_relayed()
    for dy in range(1, side):
        for dx in range(1, side):
            ggat.wait_chip(dy, dx)
            take(dy, dx)

    wide_terms = split(wbuf[...])
    u_z = []
    for i in range(1, nz):
        to = lax.rem(z + i, nz)
        rows = pl.ds(pl.multiple_of(to * h, h), h)
        ubuf[rows, :] = dot3(split(inv_t[rows, :]), wide_terms)
        u_z.append(along_z(ubuf.at[rows], rsbuf.at[i], us, ur, i))
        if i > 1:
            u_z[i - 2].start()
    rows = pl.ds(pl.multiple_of(z * h, h), h)
    ubuf[rows, :] = dot3(split(inv_t[rows, :]), wide_terms)
    u_z[-1].start()

    for copy in r_z:
        copy.wait_recv()
    pick = (iota((n, wide - k), 0) == iota((n, wide - k), 1) + c * w) & (iota((n, wide - k), 1) < w)
    r_all = jnp.concatenate([rbuf[...].reshape(n, k), pick.astype(F32)], axis=1)
    both = split(dot3(split(inv_t[...].T), split(r_all)))
    wbuf_rows = (((0,), (0,)), ((), ()))

    def out_copies(i):
        rows = pl.ds(pl.multiple_of(i * tile, tile), tile)
        return (
            pltpu.make_async_copy(tgbuf.at[rows], to_hbm.at[rows], outs.at[0, i]),
            pltpu.make_async_copy(pabuf.at[rows], pa_hbm.at[rows], outs.at[1, i]),
        )

    tp_hi[:n, :] = both[0]
    tp_lo[:n, :] = both[1]

    def trail(i, carry):
        rows = pl.ds(pl.multiple_of(i * tile, tile), tile)
        value = dot3((g_hi[:, rows], g_lo[:, rows]), (tp_hi[:n, :], tp_lo[:n, :]), wbuf_rows)
        tgbuf[rows, :] = tgbuf[rows, :] - value[:, :k]
        pabuf[rows, :] = value[:, k:k + w]
        for copy in out_copies(i):
            copy.start()
        return carry

    lax.fori_loop(0, m // tile, trail, 0)

    for copy in u_z:
        copy.wait_recv()
    total = ubuf[rows, :]
    for i in range(1, nz):
        total = total + rsbuf[i]
    rgbuf[...] = rgbuf[...] - total[:, :k]
    keep = iota((h, w), 0) + z * h >= iota((h, w), 1) + c * w
    dobuf[...] = jnp.where(keep, dgbuf[...] - total[:, k:k + w], 0.0)
    last = [
        pltpu.make_async_copy(rgbuf, ro_hbm, local.at[0]),
        pltpu.make_async_copy(dobuf, do_hbm, local.at[1]),
    ]
    for copy in last:
        copy.start()

    for copy in d_z + r_z + u_z:
        copy.wait_send()
    dgat.wait_sends()
    ggat.wait_sends()

    def drain(i, carry):
        for copy in out_copies(i):
            copy.wait()
        return carry

    lax.fori_loop(0, m // tile, drain, 0)
    for copy in last:
        copy.wait()


def on_device(nz, side, diag_factor, panel_factor, row_factor, trailing_factor, panel_grad, diag_grad, row_grad, trailing_grad):
    m, w = panel_grad.shape
    h = diag_factor.shape[0]
    k = row_factor.shape[1]
    ncol = CORES * side * side
    n = ncol * w
    wide = -(-(k + w) // 128) * 128
    dma = pltpu.SemaphoreType.DMA
    gather_sems = [
        dma((2, side)), dma((2, side)), dma((2, side, side)), dma((2, side, side)),
        dma((2, side * side)), dma((2, side * side)),
    ]
    vmem = pltpu.VMEM
    any_spec = pl.BlockSpec(memory_space=pl.ANY)
    shape = jax.ShapeDtypeStruct
    return pl.pallas_call(
        functools.partial(kernel, nz, side),
        out_shape=(shape((m, w), F32), shape((m, k), F32), shape((h, k), F32), shape((h, w), F32)),
        in_specs=[any_spec] * 8,
        out_specs=(any_spec,) * 4,
        scratch_shapes=[
            vmem((ncol, nz, w, h), F32), vmem((ncol, w, m), F32), vmem((nz, h, k), F32),
            vmem((m, k), F32), vmem((m, w), F32), vmem((h, w), F32), vmem((h, k), F32),
            vmem((m, k), F32), vmem((m, w), F32), vmem((h, w), F32),
            vmem((n, n), F32), vmem((n, n), F32),
            vmem((m, wide), BF16), vmem((m, wide), BF16),
            vmem((n, m), BF16), vmem((n, m), BF16),
            vmem((n, wide), F32), vmem((n, wide), F32), vmem((nz, h, wide), F32),
            gather_sems, list(gather_sems),
            dma((nz,)), dma((nz,)), dma((nz,)), dma((nz,)), dma((nz,)), dma((nz,)),
            dma((8,)), dma((2, m // 256)),
        ],
        compiler_params=pltpu.CompilerParams(
            collective_id=0, has_side_effects=True, vmem_limit_bytes=64000 * 1024
        ),
        name="panel_step",
    )(diag_factor.T, panel_grad.T, panel_factor, row_factor, trailing_factor, diag_grad, row_grad, trailing_grad)


def solution(mesh):
    nz, ncol = mesh.shape["row"], mesh.shape["col"]
    side = math.isqrt(ncol // CORES)
    spec = P("row", "col")
    return jax.shard_map(
        functools.partial(on_device, nz, side),
        mesh=mesh,
        in_specs=(spec,) * 8,
        out_specs=(spec,) * 4,
        check_vma=False,
    )
```

```python
import functools
import math

import jax
import jax.numpy as jnp
from jax import lax
from jax.experimental import pallas as pl
from jax.experimental.pallas import tpu as pltpu
from jax.sharding import PartitionSpec as P

MESH = pl.DeviceIdType.MESH
F32 = jnp.float32
BF16 = jnp.bfloat16
CORES = 2
VMEM_KIB = 36000


def split(x):
    hi = x.astype(BF16)
    return hi, (x - hi.astype(F32)).astype(BF16)


def dot3(a, b, dims=(((1,), (0,)), ((), ()))):
    dot = functools.partial(lax.dot_general, dimension_numbers=dims, preferred_element_type=F32)
    return dot(a[0], b[0]) + (dot(a[0], b[1]) + dot(a[1], b[0]))


def dot_high(a, b):
    return jnp.dot(a, b, precision=lax.Precision.HIGHEST, preferred_element_type=F32)


def iota(shape, dim):
    return lax.broadcasted_iota(jnp.int32, shape, dim)


def invert_base(a):
    n = a.shape[0]
    i, j = iota((n, n), 0), iota((n, n), 1)
    eye = i == j
    d = jnp.where(eye, a, 0.0)
    inv_col = 1.0 / jnp.sum(d, axis=1, keepdims=True)
    inv_row = 1.0 / jnp.sum(d, axis=0, keepdims=True)
    inv = jnp.where(eye, inv_col, 0.0)
    step = 1
    while step < n:
        pair = (i // (2 * step) == j // (2 * step)) & (i // step < j // step)
        part = jnp.where(pair, a, 0.0)
        if step == 1:
            inv = inv - part * inv_col * inv_row
        else:
            inv = inv - dot_high(dot_high(inv, part), inv)
        step *= 2
    return inv


class Gather:
    def __init__(self, place, side, buf, own, sems):
        self.z, self.y, self.x, self.core = place
        self.s, self.buf, self.own = side, buf, own
        self.p1s, self.p1r, self.p2s, self.p2r, self.cs, self.cr = sems

    def col(self, dy, dx, core):
        s = self.s
        return (lax.rem(self.y + dy + s, s) * s + lax.rem(self.x + dx + s, s)) * CORES + core

    def half(self, ref, half):
        rows = self.buf.shape[-2] // 2
        lead = (slice(None),) * (len(ref.shape) - 2)
        return ref.at[lead + (pl.ds(half * rows, rows), slice(None))]

    def block(self, dy, dx, core, half):
        return self.half(self.buf.at[self.col(dy, dx, core)], half)

    def source(self, dy, dx, half):
        if dy == 0 and dx == 0:
            return self.half(self.own, half)
        return self.block(dy, dx, self.core, half)

    def copy(self, dy, dx, half, send, recv, to):
        return pltpu.make_async_remote_copy(
            src_ref=self.source(dy, dx, half),
            dst_ref=self.block(dy, dx, self.core, half),
            send_sem=send,
            recv_sem=recv,
            device_id=(self.z, to),
            device_id_type=MESH,
        )

    def first(self, half, k):
        to = self.col(0, k, self.core) if half == 0 else self.col(k, 0, self.core)
        return self.copy(0, 0, half, self.p1s.at[half, k], self.p1r.at[half, k], to)

    def second(self, half, k, m):
        dy, dx = (0, -k) if half == 0 else (-k, 0)
        to = self.col(m, 0, self.core) if half == 0 else self.col(0, m, self.core)
        return self.copy(dy, dx, half, self.p2s.at[half, k, m], self.p2r.at[half, k, m], to)

    def across(self, dy, dx, half):
        at = dy * self.s + dx
        to = self.col(0, 0, 1 - self.core)
        return self.copy(-dy, -dx, half, self.cs.at[half, at], self.cr.at[half, at], to)

    def start_first(self):
        for k in range(1, self.s):
            for half in range(2):
                self.first(half, k).start()

    def start_own(self):
        for m in range(1, self.s):
            for half in range(2):
                self.second(half, 0, m).start()
        for half in range(2):
            self.across(0, 0, half).start()

    def relay(self):
        for k in range(1, self.s):
            for half in range(2):
                self.first(half, k).wait_recv()
                for m in range(1, self.s):
                    self.second(half, k, m).start()
                dy, dx = (0, k) if half == 0 else (k, 0)
                self.across(dy, dx, half).start()

    def pass_own(self):
        for m in range(1, self.s):
            for half in range(2):
                self.second(half, 0, m).wait_recv()
                dy, dx = (m, 0) if half == 0 else (0, m)
                self.across(dy, dx, half).start()

    def pass_relayed(self):
        for k in range(1, self.s):
            for m in range(1, self.s):
                for half in range(2):
                    self.second(half, k, m).wait_recv()
                    dy, dx = (m, k) if half == 0 else (k, m)
                    self.across(dy, dx, half).start()

    def wait_chip(self, dy, dx):
        for half in range(2):
            self.across(dy, dx, half).wait_recv()

    def wait_sends(self):
        s = self.s
        for half in range(2):
            for k in range(1, s):
                self.first(half, k).wait_send()
            for k in range(s):
                for m in range(1, s):
                    self.second(half, k, m).wait_send()
            for dy in range(s):
                for dx in range(s):
                    self.across(dy, dx, half).wait_send()


def kernel(
    nz, side, dt_hbm, gt_hbm, p_hbm, r_hbm, t_hbm, dg_hbm, rg_hbm, tg_hbm,
    pa_hbm, to_hbm, ro_hbm, do_hbm,
    dbuf, gbuf, rbuf, tbuf, pbuf, dgbuf, rgbuf, tgbuf, pabuf, dobuf,
    aup, inv_t, tp_hi, tp_lo, g_hi, g_lo, wbuf, ubuf, rsbuf,
    d_sems, g_sems, zs, zr, rs_s, rs_r, us, ur, local, outs,
):
    z = lax.axis_index("row")
    c = lax.axis_index("col")
    core = lax.rem(c, CORES)
    chip = c // CORES
    x, y = lax.rem(chip, side), chip // side
    place = (z, y, x, core)
    ncol, w, m = gbuf.shape
    n = ncol * w
    h = n // nz
    k = tbuf.shape[1]
    wide = tp_hi.shape[1]

    dgat = Gather(place, side, dbuf, dbuf.at[c], d_sems)
    ggat = Gather(place, side, gbuf, gt_hbm, g_sems)

    loads = [
        (dt_hbm, dbuf.at[c, z]),
        (t_hbm, tbuf),
        (p_hbm, pbuf),
        (gt_hbm, gbuf.at[c]),
        (r_hbm, rbuf.at[z]),
        (tg_hbm, tgbuf),
        (rg_hbm, rgbuf),
        (dg_hbm, dgbuf),
    ]
    loads = [pltpu.make_async_copy(a, b, local.at[i]) for i, (a, b) in enumerate(loads)]
    for load in loads:
        load.start()

    barrier = pltpu.get_barrier_semaphore()
    peers = [(lax.rem(z + i, nz), c) for i in range(1, nz)]
    peers += [(z, ggat.col(0, i, core)) for i in range(1, side)]
    peers += [(z, ggat.col(i, 0, core)) for i in range(1, side)]
    peers += [(z, ggat.col(0, 0, 1 - core))]
    for peer in peers:
        pl.semaphore_signal(barrier, inc=1, device_id=peer, device_id_type=MESH)
    pl.semaphore_wait(barrier, len(peers))

    def along_z(src, dst, send, recv, i):
        return pltpu.make_async_remote_copy(
            src_ref=src, dst_ref=dst, send_sem=send.at[i], recv_sem=recv.at[i],
            device_id=(lax.rem(z + i, nz), c), device_id_type=MESH,
        )

    d_z = [along_z(dt_hbm, dbuf.at[c, z], zs, zr, i) for i in range(1, nz)]
    r_z = [along_z(r_hbm, rbuf.at[z], rs_s, rs_r, i) for i in range(1, nz)]
    for copy in d_z:
        copy.start()
    ggat.start_first()
    for copy in r_z:
        copy.start()

    loads[0].wait()
    for copy in d_z:
        copy.wait_recv()
    dgat.start_first()
    dgat.start_own()

    for load in loads[1:]:
        load.wait()

    tile = 256

    def widen(i, carry):
        rows = pl.ds(pl.multiple_of(i * tile, tile), tile)
        hi, lo = split(tbuf[rows, :])
        tp_hi[rows, :k] = hi
        tp_lo[rows, :k] = lo
        tail = jnp.concatenate([pbuf[:, rows].T, jnp.zeros((tile, wide - k - w), F32)], axis=1)
        hi, lo = split(tail)
        tp_hi[rows, k:] = hi
        tp_lo[rows, k:] = lo
        return carry

    dgat.relay()
    ggat.start_own()
    ggat.relay()
    lax.fori_loop(0, m // tile, widen, 0)

    dgat.pass_own()
    dgat.pass_relayed()
    for dy in range(side):
        for dx in range(side):
            dgat.wait_chip(dy, dx)
    for col in range(ncol):
        aup[col * w:(col + 1) * w, :] = jnp.concatenate([dbuf[col, i] for i in range(nz)], axis=1)

    base = 128
    inv_t[...] = jnp.zeros((n, n), F32)
    for b in range(0, n, base):
        inv_t[b:b + base, b:b + base] = invert_base(aup[b:b + base, b:b + base])
    step = base
    while step < n:
        for b in range(0, n, 2 * step):
            up, low = slice(b, b + step), slice(b + step, b + 2 * step)
            inv_t[up, low] = -dot_high(dot_high(inv_t[up, up], aup[up, low]), inv_t[low, low])
        step *= 2

    def take(dy, dx):
        at = ggat.col(-dy, -dx, 0)
        rows = pl.ds(pl.multiple_of(at * w, CORES * w), CORES * w)
        value = split(gbuf[pl.ds(at, CORES)].reshape(CORES * w, m))
        g_hi[rows, :] = value[0]
        g_lo[rows, :] = value[1]
        wbuf[rows, :] = dot3(value, (tp_hi[...], tp_lo[...]))

    ggat.pass_own()
    ggat.wait_chip(0, 0)
    take(0, 0)
    for i in range(1, side):
        ggat.wait_chip(0, i)
        take(0, i)
        ggat.wait_chip(i, 0)
        take(i, 0)
    ggat.pass_relayed()
    for dy in range(1, side):
        for dx in range(1, side):
            ggat.wait_chip(dy, dx)
            take(dy, dx)

    wide_terms = split(wbuf[...])
    u_z = []
    for i in range(1, nz):
        to = lax.rem(z + i, nz)
        rows = pl.ds(pl.multiple_of(to * h, h), h)
        ubuf[rows, :] = dot3(split(inv_t[rows, :]), wide_terms)
        u_z.append(along_z(ubuf.at[rows], rsbuf.at[i], us, ur, i))
        if i > 1:
            u_z[i - 2].start()
    rows = pl.ds(pl.multiple_of(z * h, h), h)
    ubuf[rows, :] = dot3(split(inv_t[rows, :]), wide_terms)
    u_z[-1].start()

    for copy in r_z:
        copy.wait_recv()
    pick = (iota((n, wide - k), 0) == iota((n, wide - k), 1) + c * w) & (iota((n, wide - k), 1) < w)
    r_all = jnp.concatenate([rbuf[...].reshape(n, k), pick.astype(F32)], axis=1)
    both = split(dot3(split(inv_t[...].T), split(r_all)))
    wbuf_rows = (((0,), (0,)), ((), ()))

    def out_copies(i):
        rows = pl.ds(pl.multiple_of(i * tile, tile), tile)
        return (
            pltpu.make_async_copy(tgbuf.at[rows], to_hbm.at[rows], outs.at[0, i]),
            pltpu.make_async_copy(pabuf.at[:, rows], pa_hbm.at[:, rows], outs.at[1, i]),
        )

    tp_hi[:n, :] = both[0]
    tp_lo[:n, :] = both[1]

    def trail(i, carry):
        rows = pl.ds(pl.multiple_of(i * tile, tile), tile)
        value = dot3((g_hi[:, rows], g_lo[:, rows]), (tp_hi[:n, :], tp_lo[:n, :]), wbuf_rows)
        tgbuf[rows, :] = tgbuf[rows, :] - value[:, :k]
        pabuf[:, rows] = value[:, k:k + w].T
        for copy in out_copies(i):
            copy.start()
        return carry

    lax.fori_loop(0, m // tile, trail, 0)

    for copy in u_z:
        copy.wait_recv()
    total = ubuf[rows, :]
    for i in range(1, nz):
        total = total + rsbuf[i]
    rgbuf[...] = rgbuf[...] - total[:, :k]
    keep = iota((w, h), 1) + z * h >= iota((w, h), 0) + c * w
    dobuf[...] = jnp.where(keep, dgbuf[...] - total[:, k:k + w].T, 0.0)
    last = [
        pltpu.make_async_copy(rgbuf, ro_hbm, local.at[0]),
        pltpu.make_async_copy(dobuf, do_hbm, local.at[1]),
    ]
    for copy in last:
        copy.start()

    for copy in d_z + r_z + u_z:
        copy.wait_send()
    dgat.wait_sends()
    ggat.wait_sends()

    def drain(i, carry):
        for copy in out_copies(i):
            copy.wait()
        return carry

    lax.fori_loop(0, m // tile, drain, 0)
    for copy in last:
        copy.wait()


def on_device(nz, side, diag_factor, panel_factor, row_factor, trailing_factor, panel_grad, diag_grad, row_grad, trailing_grad):
    m, w = panel_grad.shape
    h = diag_factor.shape[0]
    k = row_factor.shape[1]
    ncol = CORES * side * side
    n = ncol * w
    wide = -(-(k + w) // 128) * 128
    dma = pltpu.SemaphoreType.DMA
    gather_sems = [
        dma((2, side)), dma((2, side)), dma((2, side, side)), dma((2, side, side)),
        dma((2, side * side)), dma((2, side * side)),
    ]
    vmem = pltpu.VMEM
    any_spec = pl.BlockSpec(memory_space=pl.ANY)
    shape = jax.ShapeDtypeStruct
    operands = (
        diag_factor.T, panel_grad.T, panel_factor.T, row_factor,
        trailing_factor, diag_grad.T, row_grad, trailing_grad,
    )
    pa, to, ro, do = pl.pallas_call(
        functools.partial(kernel, nz, side),
        out_shape=(shape((w, m), F32), shape((m, k), F32), shape((h, k), F32), shape((w, h), F32)),
        in_specs=[pl.BlockSpec(memory_space=pltpu.HBM)] * 8,
        out_specs=(any_spec,) * 4,
        scratch_shapes=[
            vmem((ncol, nz, w, h), F32), vmem((ncol, w, m), F32), vmem((nz, h, k), F32),
            vmem((m, k), F32), vmem((w, m), F32), vmem((w, h), F32), vmem((h, k), F32),
            vmem((m, k), F32), vmem((w, m), F32), vmem((w, h), F32),
            vmem((n, n), F32), vmem((n, n), F32),
            vmem((m, wide), BF16), vmem((m, wide), BF16),
            vmem((n, m), BF16), vmem((n, m), BF16),
            vmem((n, wide), F32), vmem((n, wide), F32), vmem((nz, h, wide), F32),
            gather_sems, list(gather_sems),
            dma((nz,)), dma((nz,)), dma((nz,)), dma((nz,)), dma((nz,)), dma((nz,)),
            dma((8,)), dma((2, m // 256)),
        ],
        compiler_params=pltpu.CompilerParams(
            collective_id=0, has_side_effects=True, vmem_limit_bytes=VMEM_KIB * 1024
        ),
        name="panel_step",
    )(*(pltpu.with_memory_space_constraint(v, pltpu.HBM) for v in operands))
    return pa.T, to, ro, do.T


def solution(mesh):
    nz, ncol = mesh.shape["row"], mesh.shape["col"]
    side = math.isqrt(ncol // CORES)
    spec = P("row", "col")
    return jax.shard_map(
        functools.partial(on_device, nz, side),
        mesh=mesh,
        in_specs=(spec,) * 8,
        out_specs=(spec,) * 4,
        check_vma=False,
    )
```

```python
import functools
import math

import jax
import jax.numpy as jnp
from jax import lax
from jax.experimental import pallas as pl
from jax.experimental.pallas import tpu as pltpu
from jax.sharding import PartitionSpec as P

MESH = pl.DeviceIdType.MESH
F32 = jnp.float32
BF16 = jnp.bfloat16
CORES = 2
VMEM_KIB = 36000


def split(x):
    hi = x.astype(BF16)
    return hi, (x - hi.astype(F32)).astype(BF16)


def dot3(a, b, dims=(((1,), (0,)), ((), ()))):
    dot = functools.partial(lax.dot_general, dimension_numbers=dims, preferred_element_type=F32)
    return dot(a[0], b[0]) + (dot(a[0], b[1]) + dot(a[1], b[0]))


def dot_high(a, b):
    return jnp.dot(a, b, precision=lax.Precision.HIGHEST, preferred_element_type=F32)


def iota(shape, dim):
    return lax.broadcasted_iota(jnp.int32, shape, dim)


def invert_bases(blocks):
    n = blocks[0].shape[0]
    i, j = iota((n, n), 0), iota((n, n), 1)
    eye = i == j
    diag = [jnp.where(eye, a, 0.0) for a in blocks]
    cols = [1.0 / jnp.sum(d, axis=1, keepdims=True) for d in diag]
    rows = [1.0 / jnp.sum(d, axis=0, keepdims=True) for d in diag]
    invs = [jnp.where(eye, col, 0.0) for col in cols]
    step = 1
    while step < n:
        pair = (i // (2 * step) == j // (2 * step)) & (i // step < j // step)
        parts = [jnp.where(pair, a, 0.0) for a in blocks]
        if step == 1:
            invs = [inv - part * col * row for inv, part, col, row in zip(invs, parts, cols, rows)]
        else:
            mids = [dot_high(inv, part) for inv, part in zip(invs, parts)]
            ends = [dot_high(mid, inv) for mid, inv in zip(mids, invs)]
            invs = [inv - end for inv, end in zip(invs, ends)]
        step *= 2
    return invs


class Gather:
    def __init__(self, place, side, buf, own, sems):
        self.z, self.y, self.x, self.core = place
        self.s, self.buf, self.own = side, buf, own
        self.p1s, self.p1r, self.p2s, self.p2r, self.cs, self.cr = sems

    def col(self, dy, dx, core):
        s = self.s
        return (lax.rem(self.y + dy + s, s) * s + lax.rem(self.x + dx + s, s)) * CORES + core

    def half(self, ref, half):
        rows = self.buf.shape[-2] // 2
        lead = (slice(None),) * (len(ref.shape) - 2)
        return ref.at[lead + (pl.ds(half * rows, rows), slice(None))]

    def block(self, dy, dx, core, half):
        return self.half(self.buf.at[self.col(dy, dx, core)], half)

    def source(self, dy, dx, half):
        if dy == 0 and dx == 0:
            return self.half(self.own, half)
        return self.block(dy, dx, self.core, half)

    def copy(self, dy, dx, half, send, recv, to):
        return pltpu.make_async_remote_copy(
            src_ref=self.source(dy, dx, half),
            dst_ref=self.block(dy, dx, self.core, half),
            send_sem=send,
            recv_sem=recv,
            device_id=(self.z, to),
            device_id_type=MESH,
        )

    def first(self, half, k):
        to = self.col(0, k, self.core) if half == 0 else self.col(k, 0, self.core)
        return self.copy(0, 0, half, self.p1s.at[half, k], self.p1r.at[half, k], to)

    def second(self, half, k, m):
        dy, dx = (0, -k) if half == 0 else (-k, 0)
        to = self.col(m, 0, self.core) if half == 0 else self.col(0, m, self.core)
        return self.copy(dy, dx, half, self.p2s.at[half, k, m], self.p2r.at[half, k, m], to)

    def across(self, dy, dx, half):
        at = dy * self.s + dx
        to = self.col(0, 0, 1 - self.core)
        return self.copy(-dy, -dx, half, self.cs.at[half, at], self.cr.at[half, at], to)

    def start_first(self):
        for k in range(1, self.s):
            for half in range(2):
                self.first(half, k).start()

    def start_own(self):
        for m in range(1, self.s):
            for half in range(2):
                self.second(half, 0, m).start()
        for half in range(2):
            self.across(0, 0, half).start()

    def relay(self):
        for k in range(1, self.s):
            for half in range(2):
                self.first(half, k).wait_recv()
                for m in range(1, self.s):
                    self.second(half, k, m).start()
                dy, dx = (0, k) if half == 0 else (k, 0)
                self.across(dy, dx, half).start()

    def pass_own(self):
        for m in range(1, self.s):
            for half in range(2):
                self.second(half, 0, m).wait_recv()
                dy, dx = (m, 0) if half == 0 else (0, m)
                self.across(dy, dx, half).start()

    def pass_relayed(self):
        for k in range(1, self.s):
            for m in range(1, self.s):
                for half in range(2):
                    self.second(half, k, m).wait_recv()
                    dy, dx = (m, k) if half == 0 else (k, m)
                    self.across(dy, dx, half).start()

    def wait_chip(self, dy, dx):
        for half in range(2):
            self.across(dy, dx, half).wait_recv()

    def wait_sends(self):
        s = self.s
        for half in range(2):
            for k in range(1, s):
                self.first(half, k).wait_send()
            for k in range(s):
                for m in range(1, s):
                    self.second(half, k, m).wait_send()
            for dy in range(s):
                for dx in range(s):
                    self.across(dy, dx, half).wait_send()


def kernel(
    nz, side, dt_hbm, gt_hbm, p_hbm, r_hbm, t_hbm, dg_hbm, rg_hbm, tg_hbm,
    pa_hbm, to_hbm, ro_hbm, do_hbm,
    dbuf, gbuf, rbuf, tbuf, pbuf, dgbuf, rgbuf, tgbuf, pabuf, dobuf,
    aup, inv_t, tp_hi, tp_lo, g_hi, g_lo, wbuf, ubuf, vbuf, rsbuf, rvbuf,
    d_sems, g_sems, zs, zr, rs_s, rs_r, us, ur, vs, vr, local, outs,
):
    z = lax.axis_index("row")
    c = lax.axis_index("col")
    core = lax.rem(c, CORES)
    chip = c // CORES
    x, y = lax.rem(chip, side), chip // side
    place = (z, y, x, core)
    ncol, w, m = gbuf.shape
    n = ncol * w
    h = n // nz
    k = tbuf.shape[1]
    wide = tp_hi.shape[1]

    dgat = Gather(place, side, dbuf, dbuf.at[c], d_sems)
    ggat = Gather(place, side, gbuf, gt_hbm, g_sems)

    loads = [
        (dt_hbm, dbuf.at[c, z]),
        (t_hbm, tbuf),
        (p_hbm, pbuf),
        (gt_hbm, gbuf.at[c]),
        (r_hbm, rbuf.at[z]),
        (tg_hbm, tgbuf),
        (rg_hbm, rgbuf),
        (dg_hbm, dgbuf),
    ]
    loads = [pltpu.make_async_copy(a, b, local.at[i]) for i, (a, b) in enumerate(loads)]
    for load in loads:
        load.start()

    barrier = pltpu.get_barrier_semaphore()
    peers = [(lax.rem(z + i, nz), c) for i in range(1, nz)]
    peers += [(z, ggat.col(0, i, core)) for i in range(1, side)]
    peers += [(z, ggat.col(i, 0, core)) for i in range(1, side)]
    peers += [(z, ggat.col(0, 0, 1 - core))]
    for peer in peers:
        pl.semaphore_signal(barrier, inc=1, device_id=peer, device_id_type=MESH)
    pl.semaphore_wait(barrier, len(peers))

    def along_z(src, dst, send, recv, i):
        return pltpu.make_async_remote_copy(
            src_ref=src, dst_ref=dst, send_sem=send.at[i], recv_sem=recv.at[i],
            device_id=(lax.rem(z + i, nz), c), device_id_type=MESH,
        )

    d_z = [along_z(dt_hbm, dbuf.at[c, z], zs, zr, i) for i in range(1, nz)]
    r_z = [along_z(r_hbm, rbuf.at[z], rs_s, rs_r, i) for i in range(1, nz)]
    for copy in d_z:
        copy.start()
    ggat.start_first()
    for copy in r_z:
        copy.start()

    loads[0].wait()
    for copy in d_z:
        copy.wait_recv()
    dgat.start_first()
    dgat.start_own()

    tile = 256

    def widen(i, carry):
        rows = pl.ds(pl.multiple_of(i * tile, tile), tile)
        hi, lo = split(tbuf[rows, :])
        tp_hi[rows, :k] = hi
        tp_lo[rows, :k] = lo
        tail = jnp.concatenate([pbuf[:, rows].T, jnp.zeros((tile, wide - k - w), F32)], axis=1)
        hi, lo = split(tail)
        tp_hi[rows, k:] = hi
        tp_lo[rows, k:] = lo
        return carry

    for load in loads[1:3]:
        load.wait()
    lax.fori_loop(0, m // tile, widen, 0)
    dgat.relay()
    ggat.start_own()
    ggat.relay()
    dgat.pass_own()
    dgat.pass_relayed()

    def take(dy, dx):
        at = ggat.col(-dy, -dx, 0)
        rows = pl.ds(pl.multiple_of(at * w, CORES * w), CORES * w)
        value = split(gbuf[pl.ds(at, CORES)].reshape(CORES * w, m))
        g_hi[rows, :] = value[0]
        g_lo[rows, :] = value[1]
        wbuf[rows, :] = dot3(value, (tp_hi[...], tp_lo[...]))

    for load in loads[3:]:
        load.wait()
    ggat.wait_chip(0, 0)
    take(0, 0)
    for dy in range(side):
        for dx in range(side):
            dgat.wait_chip(dy, dx)
    for col in range(ncol):
        aup[col * w:(col + 1) * w, :] = jnp.concatenate([dbuf[col, i] for i in range(nz)], axis=1)

    base = 128
    inv_t[...] = jnp.zeros((n, n), F32)
    starts = range(0, n, base)
    bases = invert_bases([aup[b:b + base, b:b + base] for b in starts])
    for b, inv in zip(starts, bases):
        inv_t[b:b + base, b:b + base] = inv
    ggat.pass_own()
    step = base
    while step < n:
        for b in range(0, n, 2 * step):
            up, low = slice(b, b + step), slice(b + step, b + 2 * step)
            inv_t[up, low] = -dot_high(dot_high(inv_t[up, up], aup[up, low]), inv_t[low, low])
        step *= 2

    for i in range(1, side):
        ggat.wait_chip(0, i)
        take(0, i)
        ggat.wait_chip(i, 0)
        take(i, 0)
    ggat.pass_relayed()
    for dy in range(1, side):
        for dx in range(1, side):
            ggat.wait_chip(dy, dx)
            take(dy, dx)

    wide_terms = split(wbuf[...])
    u_z = []

    def terms(i):
        to = lax.rem(z + i, nz)
        rows = pl.ds(pl.multiple_of(to * h, h), h)
        value = dot3(split(inv_t[rows, :]), wide_terms)
        ubuf[i] = value[:, :k]
        vbuf[i] = value[:, k:k + w].T

    order = sorted(range(1, nz), key=lambda i: -min(i, nz - i))
    for at, i in enumerate(order):
        terms(i)
        u_z.append((
            along_z(ubuf.at[i], rsbuf.at[i], us, ur, i),
            along_z(vbuf.at[i], rvbuf.at[i], vs, vr, i),
        ))
        if at > 0:
            for copy in u_z[at - 1]:
                copy.start()
    terms(0)
    for copy in u_z[-1]:
        copy.start()
    u_z = [copy for pair in u_z for copy in pair]

    for copy in r_z:
        copy.wait_recv()
    pick = (iota((n, wide - k), 0) == iota((n, wide - k), 1) + c * w) & (iota((n, wide - k), 1) < w)
    r_all = jnp.concatenate([rbuf[...].reshape(n, k), pick.astype(F32)], axis=1)
    both = split(dot3(split(inv_t[...].T), split(r_all)))
    wbuf_rows = (((0,), (0,)), ((), ()))

    def out_copies(i):
        rows = pl.ds(pl.multiple_of(i * tile, tile), tile)
        return (
            pltpu.make_async_copy(tgbuf.at[rows], to_hbm.at[rows], outs.at[0, i]),
            pltpu.make_async_copy(pabuf.at[:, rows], pa_hbm.at[:, rows], outs.at[1, i]),
        )

    tp_hi[:n, :] = both[0]
    tp_lo[:n, :] = both[1]

    def trail(i, carry):
        rows = pl.ds(pl.multiple_of(i * tile, tile), tile)
        value = dot3((g_hi[:, rows], g_lo[:, rows]), (tp_hi[:n, :], tp_lo[:n, :]), wbuf_rows)
        tgbuf[rows, :] = tgbuf[rows, :] - value[:, :k]
        pabuf[:, rows] = value[:, k:k + w].T
        for copy in out_copies(i):
            copy.start()
        return carry

    lax.fori_loop(0, m // tile, trail, 0)

    for copy in u_z:
        copy.wait_recv()
    row_sum, diag_sum = ubuf[0], vbuf[0]
    for i in range(1, nz):
        row_sum = row_sum + rsbuf[i]
        diag_sum = diag_sum + rvbuf[i]
    rgbuf[...] = rgbuf[...] - row_sum
    keep = iota((w, h), 1) + z * h >= iota((w, h), 0) + c * w
    dobuf[...] = jnp.where(keep, dgbuf[...] - diag_sum, 0.0)
    last = [
        pltpu.make_async_copy(rgbuf, ro_hbm, local.at[0]),
        pltpu.make_async_copy(dobuf, do_hbm, local.at[1]),
    ]
    for copy in last:
        copy.start()

    for copy in d_z + r_z + u_z:
        copy.wait_send()
    dgat.wait_sends()
    ggat.wait_sends()

    def drain(i, carry):
        for copy in out_copies(i):
            copy.wait()
        return carry

    lax.fori_loop(0, m // tile, drain, 0)
    for copy in last:
        copy.wait()


def on_device(nz, side, diag_factor, panel_factor, row_factor, trailing_factor, panel_grad, diag_grad, row_grad, trailing_grad):
    m, w = panel_grad.shape
    h = diag_factor.shape[0]
    k = row_factor.shape[1]
    ncol = CORES * side * side
    n = ncol * w
    wide = -(-(k + w) // 128) * 128
    dma = pltpu.SemaphoreType.DMA
    gather_sems = [
        dma((2, side)), dma((2, side)), dma((2, side, side)), dma((2, side, side)),
        dma((2, side * side)), dma((2, side * side)),
    ]
    vmem = pltpu.VMEM
    any_spec = pl.BlockSpec(memory_space=pl.ANY)
    shape = jax.ShapeDtypeStruct
    operands = (
        diag_factor.T, panel_grad.T, panel_factor.T, row_factor,
        trailing_factor, diag_grad.T, row_grad, trailing_grad,
    )
    pa, to, ro, do = pl.pallas_call(
        functools.partial(kernel, nz, side),
        out_shape=(shape((w, m), F32), shape((m, k), F32), shape((h, k), F32), shape((w, h), F32)),
        in_specs=[pl.BlockSpec(memory_space=pltpu.HBM)] * 8,
        out_specs=(any_spec,) * 4,
        scratch_shapes=[
            vmem((ncol, nz, w, h), F32), vmem((ncol, w, m), F32), vmem((nz, h, k), F32),
            vmem((m, k), F32), vmem((w, m), F32), vmem((w, h), F32), vmem((h, k), F32),
            vmem((m, k), F32), vmem((w, m), F32), vmem((w, h), F32),
            vmem((n, n), F32), vmem((n, n), F32),
            vmem((m, wide), BF16), vmem((m, wide), BF16),
            vmem((n, m), BF16), vmem((n, m), BF16),
            vmem((n, wide), F32), vmem((nz, h, k), F32), vmem((nz, w, h), F32),
            vmem((nz, h, k), F32), vmem((nz, w, h), F32),
            gather_sems, list(gather_sems),
            *[dma((nz,)) for _ in range(8)],
            dma((8,)), dma((2, m // 256)),
        ],
        compiler_params=pltpu.CompilerParams(
            collective_id=0, has_side_effects=True, vmem_limit_bytes=VMEM_KIB * 1024
        ),
        name="panel_step",
    )(*(pltpu.with_memory_space_constraint(v, pltpu.HBM) for v in operands))
    return pa.T, to, ro, do.T


def solution(mesh):
    nz, ncol = mesh.shape["row"], mesh.shape["col"]
    side = math.isqrt(ncol // CORES)
    spec = P("row", "col")
    return jax.shard_map(
        functools.partial(on_device, nz, side),
        mesh=mesh,
        in_specs=(spec,) * 8,
        out_specs=(spec,) * 4,
        check_vma=False,
    )
```

```python
import functools
import math

import jax
import jax.numpy as jnp
from jax import lax
from jax.experimental import pallas as pl
from jax.experimental.pallas import tpu as pltpu
from jax.sharding import PartitionSpec as P

MESH = pl.DeviceIdType.MESH
F32 = jnp.float32
BF16 = jnp.bfloat16
CORES = 2
VMEM_KIB = 36000


def split(x):
    hi = x.astype(BF16)
    return hi, (x - hi.astype(F32)).astype(BF16)


def dot3(a, b, dims=(((1,), (0,)), ((), ()))):
    dot = functools.partial(lax.dot_general, dimension_numbers=dims, preferred_element_type=F32)
    return dot(a[0], b[0]) + (dot(a[0], b[1]) + dot(a[1], b[0]))


def dot_high(a, b):
    return jnp.dot(a, b, precision=lax.Precision.HIGHEST, preferred_element_type=F32)


def iota(shape, dim):
    return lax.broadcasted_iota(jnp.int32, shape, dim)


def invert_bases(blocks):
    n = blocks[0].shape[0]
    i, j = iota((n, n), 0), iota((n, n), 1)
    eye = i == j
    diag = [jnp.where(eye, a, 0.0) for a in blocks]
    cols = [1.0 / jnp.sum(d, axis=1, keepdims=True) for d in diag]
    rows = [1.0 / jnp.sum(d, axis=0, keepdims=True) for d in diag]
    invs = [jnp.where(eye, col, 0.0) for col in cols]
    step = 1
    while step < n:
        pair = (i // (2 * step) == j // (2 * step)) & (i // step < j // step)
        parts = [jnp.where(pair, a, 0.0) for a in blocks]
        if step == 1:
            invs = [inv - part * col * row for inv, part, col, row in zip(invs, parts, cols, rows)]
        else:
            mids = [dot_high(inv, part) for inv, part in zip(invs, parts)]
            ends = [dot_high(mid, inv) for mid, inv in zip(mids, invs)]
            invs = [inv - end for inv, end in zip(invs, ends)]
        step *= 2
    return invs


class Gather:
    def __init__(self, place, side, buf, own, sems):
        self.z, self.y, self.x, self.core = place
        self.s, self.buf, self.own = side, buf, own
        self.p1s, self.p1r, self.p2s, self.p2r, self.cs, self.cr = sems

    def col(self, dy, dx, core):
        s = self.s
        return (lax.rem(self.y + dy + s, s) * s + lax.rem(self.x + dx + s, s)) * CORES + core

    def half(self, ref, half):
        rows = self.buf.shape[-2] // 2
        lead = (slice(None),) * (len(ref.shape) - 2)
        return ref.at[lead + (pl.ds(half * rows, rows), slice(None))]

    def block(self, dy, dx, core, half):
        return self.half(self.buf.at[self.col(dy, dx, core)], half)

    def source(self, dy, dx, half):
        if dy == 0 and dx == 0:
            return self.half(self.own, half)
        return self.block(dy, dx, self.core, half)

    def copy(self, dy, dx, half, send, recv, to):
        return pltpu.make_async_remote_copy(
            src_ref=self.source(dy, dx, half),
            dst_ref=self.block(dy, dx, self.core, half),
            send_sem=send,
            recv_sem=recv,
            device_id=(self.z, to),
            device_id_type=MESH,
        )

    def first(self, half, k):
        to = self.col(0, k, self.core) if half == 0 else self.col(k, 0, self.core)
        return self.copy(0, 0, half, self.p1s.at[half, k], self.p1r.at[half, k], to)

    def second(self, half, k, m):
        dy, dx = (0, -k) if half == 0 else (-k, 0)
        to = self.col(m, 0, self.core) if half == 0 else self.col(0, m, self.core)
        return self.copy(dy, dx, half, self.p2s.at[half, k, m], self.p2r.at[half, k, m], to)

    def across(self, dy, dx, half):
        at = dy * self.s + dx
        to = self.col(0, 0, 1 - self.core)
        return self.copy(-dy, -dx, half, self.cs.at[half, at], self.cr.at[half, at], to)

    def start_first(self):
        for k in range(1, self.s):
            for half in range(2):
                self.first(half, k).start()

    def start_own(self):
        for m in range(1, self.s):
            for half in range(2):
                self.second(half, 0, m).start()
        for half in range(2):
            self.across(0, 0, half).start()

    def relay(self):
        for k in range(1, self.s):
            for half in range(2):
                self.first(half, k).wait_recv()
                for m in range(1, self.s):
                    self.second(half, k, m).start()
                dy, dx = (0, k) if half == 0 else (k, 0)
                self.across(dy, dx, half).start()

    def pass_own(self):
        for m in range(1, self.s):
            for half in range(2):
                self.second(half, 0, m).wait_recv()
                dy, dx = (m, 0) if half == 0 else (0, m)
                self.across(dy, dx, half).start()

    def pass_relayed(self):
        for k in range(1, self.s):
            for m in range(1, self.s):
                for half in range(2):
                    self.second(half, k, m).wait_recv()
                    dy, dx = (m, k) if half == 0 else (k, m)
                    self.across(dy, dx, half).start()

    def wait_chip(self, dy, dx):
        for half in range(2):
            self.across(dy, dx, half).wait_recv()

    def wait_sends(self):
        s = self.s
        for half in range(2):
            for k in range(1, s):
                self.first(half, k).wait_send()
            for k in range(s):
                for m in range(1, s):
                    self.second(half, k, m).wait_send()
            for dy in range(s):
                for dx in range(s):
                    self.across(dy, dx, half).wait_send()


def kernel(
    nz, side, dt_hbm, gt_hbm, p_hbm, r_hbm, t_hbm, dg_hbm, rg_hbm, tg_hbm,
    pa_hbm, to_hbm, ro_hbm, do_hbm,
    dbuf, gbuf, rbuf, tbuf, pbuf, dgbuf, rgbuf, tgbuf, pabuf, dobuf,
    aup, inv_t, tp_hi, tp_lo, g_hi, g_lo, wbuf, ubuf, vbuf, rsbuf, rvbuf,
    d_sems, g_sems, zs, zr, rs_s, rs_r, us, ur, vs, vr, local, outs,
):
    z = lax.axis_index("row")
    c = lax.axis_index("col")
    core = lax.rem(c, CORES)
    chip = c // CORES
    x, y = lax.rem(chip, side), chip // side
    place = (z, y, x, core)
    ncol, w, m = gbuf.shape
    n = ncol * w
    h = n // nz
    k = tbuf.shape[1]
    wide = tp_hi.shape[1]

    dgat = Gather(place, side, dbuf, dbuf.at[c], d_sems)
    ggat = Gather(place, side, gbuf, gt_hbm, g_sems)

    loads = [
        (dt_hbm, dbuf.at[c, z]),
        (t_hbm, tbuf),
        (p_hbm, pbuf),
        (gt_hbm, gbuf.at[c]),
        (r_hbm, rbuf.at[z]),
        (tg_hbm, tgbuf),
        (rg_hbm, rgbuf),
        (dg_hbm, dgbuf),
    ]
    loads = [pltpu.make_async_copy(a, b, local.at[i]) for i, (a, b) in enumerate(loads)]
    for load in loads:
        load.start()

    barrier = pltpu.get_barrier_semaphore()
    peers = [(lax.rem(z + i, nz), c) for i in range(1, nz)]
    peers += [(z, ggat.col(0, i, core)) for i in range(1, side)]
    peers += [(z, ggat.col(i, 0, core)) for i in range(1, side)]
    peers += [(z, ggat.col(0, 0, 1 - core))]
    for peer in peers:
        pl.semaphore_signal(barrier, inc=1, device_id=peer, device_id_type=MESH)
    pl.semaphore_wait(barrier, len(peers))

    def along_z(src, dst, send, recv, i):
        return pltpu.make_async_remote_copy(
            src_ref=src, dst_ref=dst, send_sem=send.at[i], recv_sem=recv.at[i],
            device_id=(lax.rem(z + i, nz), c), device_id_type=MESH,
        )

    d_z = [along_z(dt_hbm, dbuf.at[c, z], zs, zr, i) for i in range(1, nz)]
    r_z = [along_z(r_hbm, rbuf.at[z], rs_s, rs_r, i) for i in range(1, nz)]
    for copy in d_z:
        copy.start()
    ggat.start_first()
    for copy in r_z:
        copy.start()

    loads[0].wait()
    for copy in d_z:
        copy.wait_recv()
    dgat.start_first()
    dgat.start_own()

    tile = 256

    def widen(i, carry):
        rows = pl.ds(pl.multiple_of(i * tile, tile), tile)
        hi, lo = split(tbuf[rows, :])
        tp_hi[rows, :k] = hi
        tp_lo[rows, :k] = lo
        tail = jnp.concatenate([pbuf[:, rows].T, jnp.zeros((tile, wide - k - w), F32)], axis=1)
        hi, lo = split(tail)
        tp_hi[rows, k:] = hi
        tp_lo[rows, k:] = lo
        return carry

    for load in loads[1:3]:
        load.wait()
    lax.fori_loop(0, m // tile, widen, 0)
    dgat.relay()
    ggat.start_own()
    ggat.relay()
    dgat.pass_own()
    dgat.pass_relayed()

    def take(dy, dx):
        at = ggat.col(-dy, -dx, 0)
        rows = pl.ds(pl.multiple_of(at * w, CORES * w), CORES * w)
        value = split(gbuf[pl.ds(at, CORES)].reshape(CORES * w, m))
        g_hi[rows, :] = value[0]
        g_lo[rows, :] = value[1]
        wbuf[rows, :] = dot3(value, (tp_hi[...], tp_lo[...]))

    for load in loads[3:]:
        load.wait()
    ggat.wait_chip(0, 0)
    take(0, 0)
    for dy in range(side):
        for dx in range(side):
            dgat.wait_chip(dy, dx)
    for col in range(ncol):
        aup[col * w:(col + 1) * w, :] = jnp.concatenate([dbuf[col, i] for i in range(nz)], axis=1)

    base = 128
    inv_t[...] = jnp.zeros((n, n), F32)
    starts = range(0, n, base)
    bases = invert_bases([aup[b:b + base, b:b + base] for b in starts])
    for b, inv in zip(starts, bases):
        inv_t[b:b + base, b:b + base] = inv
    ggat.pass_own()
    step = base
    while step < n:
        for b in range(0, n, 2 * step):
            up, low = slice(b, b + step), slice(b + step, b + 2 * step)
            inv_t[up, low] = -dot_high(dot_high(inv_t[up, up], aup[up, low]), inv_t[low, low])
        step *= 2

    for i in range(1, side):
        ggat.wait_chip(0, i)
        take(0, i)
        ggat.wait_chip(i, 0)
        take(i, 0)
    ggat.pass_relayed()
    for dy in range(1, side):
        for dx in range(1, side):
            ggat.wait_chip(dy, dx)
            take(dy, dx)

    wide_terms = split(wbuf[...])
    u_z = []

    def terms(i, to):
        rows = pl.ds(pl.multiple_of(to * h, h), h)
        value = dot3(split(inv_t[rows, :]), wide_terms)
        ubuf[i] = value[:, :k]
        vbuf[i] = value[:, k:k + w].T

    def to_row(i, slot, to):
        return [
            pltpu.make_async_remote_copy(
                src_ref=src.at[i], dst_ref=dst.at[slot], send_sem=send.at[i], recv_sem=recv.at[slot],
                device_id=(to, c), device_id_type=MESH,
            )
            for src, dst, send, recv in ((ubuf, rsbuf, us, ur), (vbuf, rvbuf, vs, vr))
        ]

    joined = nz == 4
    if joined:
        end = (z == 0) | (z == nz - 1)
        low = z < 2
        partner = z + 1 - 2 * lax.rem(z, 2)
        middle, far = jnp.where(low, 2, 1), jnp.where(low, nz - 1, 0)
        near_z = to_row(1, 1, partner)
        middle_z = to_row(2, jnp.where(end, 2, 3), middle)
        far_z = to_row(3, jnp.where(end, 0, 2), jnp.where(end, partner, far))
        terms(3, far)
        terms(2, middle)

        @pl.when(end)
        def _():
            for copy in far_z:
                copy.start()

        terms(1, partner)
        for copy in middle_z:
            copy.start()
        terms(0, z)
        for copy in near_z:
            copy.start()
        u_z = near_z + middle_z + far_z
    else:
        order = sorted(range(1, nz), key=lambda i: -min(i, nz - i))
        for at, i in enumerate(order):
            to = lax.rem(z + i, nz)
            terms(i, to)
            u_z.append(to_row(i, i, to))
            if at > 0:
                for copy in u_z[at - 1]:
                    copy.start()
        terms(0, z)
        for copy in u_z[-1]:
            copy.start()
        u_z = [copy for pair in u_z for copy in pair]

    for copy in r_z:
        copy.wait_recv()
    pick = (iota((n, wide - k), 0) == iota((n, wide - k), 1) + c * w) & (iota((n, wide - k), 1) < w)
    r_all = jnp.concatenate([rbuf[...].reshape(n, k), pick.astype(F32)], axis=1)
    both = split(dot3(split(inv_t[...].T), split(r_all)))
    wbuf_rows = (((0,), (0,)), ((), ()))

    def out_copies(i):
        rows = pl.ds(pl.multiple_of(i * tile, tile), tile)
        return (
            pltpu.make_async_copy(tgbuf.at[rows], to_hbm.at[rows], outs.at[0, i]),
            pltpu.make_async_copy(pabuf.at[:, rows], pa_hbm.at[:, rows], outs.at[1, i]),
        )

    tp_hi[:n, :] = both[0]
    tp_lo[:n, :] = both[1]

    if joined:
        @pl.when(jnp.logical_not(end))
        def _():
            for copy in to_row(3, 0, partner):
                copy.wait_recv()
            ubuf[3] = ubuf[3] + rsbuf[0]
            vbuf[3] = vbuf[3] + rvbuf[0]
            for copy in far_z:
                copy.start()

    def trail(i, carry):
        rows = pl.ds(pl.multiple_of(i * tile, tile), tile)
        value = dot3((g_hi[:, rows], g_lo[:, rows]), (tp_hi[:n, :], tp_lo[:n, :]), wbuf_rows)
        tgbuf[rows, :] = tgbuf[rows, :] - value[:, :k]
        pabuf[:, rows] = value[:, k:k + w].T
        for copy in out_copies(i):
            copy.start()
        return carry

    lax.fori_loop(0, m // tile, trail, 0)

    if joined:
        @pl.when(jnp.logical_not(end))
        def _():
            for copy in to_row(3, 3, partner):
                copy.wait_recv()
            ubuf[0] = ubuf[0] + rsbuf[3]
            vbuf[0] = vbuf[0] + rvbuf[3]

        for copy in to_row(1, 1, partner) + to_row(2, 2, partner):
            copy.wait_recv()
    else:
        for copy in u_z:
            copy.wait_recv()
    row_sum, diag_sum = ubuf[0], vbuf[0]
    for i in range(1, 3 if joined else nz):
        row_sum = row_sum + rsbuf[i]
        diag_sum = diag_sum + rvbuf[i]
    rgbuf[...] = rgbuf[...] - row_sum
    keep = iota((w, h), 1) + z * h >= iota((w, h), 0) + c * w
    dobuf[...] = jnp.where(keep, dgbuf[...] - diag_sum, 0.0)
    last = [
        pltpu.make_async_copy(rgbuf, ro_hbm, local.at[0]),
        pltpu.make_async_copy(dobuf, do_hbm, local.at[1]),
    ]
    for copy in last:
        copy.start()

    for copy in d_z + r_z + u_z:
        copy.wait_send()
    dgat.wait_sends()
    ggat.wait_sends()

    def drain(i, carry):
        for copy in out_copies(i):
            copy.wait()
        return carry

    lax.fori_loop(0, m // tile, drain, 0)
    for copy in last:
        copy.wait()


def on_device(nz, side, diag_factor, panel_factor, row_factor, trailing_factor, panel_grad, diag_grad, row_grad, trailing_grad):
    m, w = panel_grad.shape
    h = diag_factor.shape[0]
    k = row_factor.shape[1]
    ncol = CORES * side * side
    n = ncol * w
    wide = -(-(k + w) // 128) * 128
    dma = pltpu.SemaphoreType.DMA
    gather_sems = [
        dma((2, side)), dma((2, side)), dma((2, side, side)), dma((2, side, side)),
        dma((2, side * side)), dma((2, side * side)),
    ]
    vmem = pltpu.VMEM
    any_spec = pl.BlockSpec(memory_space=pl.ANY)
    shape = jax.ShapeDtypeStruct
    operands = (
        diag_factor.T, panel_grad.T, panel_factor.T, row_factor,
        trailing_factor, diag_grad.T, row_grad, trailing_grad,
    )
    pa, to, ro, do = pl.pallas_call(
        functools.partial(kernel, nz, side),
        out_shape=(shape((w, m), F32), shape((m, k), F32), shape((h, k), F32), shape((w, h), F32)),
        in_specs=[pl.BlockSpec(memory_space=pltpu.HBM)] * 8,
        out_specs=(any_spec,) * 4,
        scratch_shapes=[
            vmem((ncol, nz, w, h), F32), vmem((ncol, w, m), F32), vmem((nz, h, k), F32),
            vmem((m, k), F32), vmem((w, m), F32), vmem((w, h), F32), vmem((h, k), F32),
            vmem((m, k), F32), vmem((w, m), F32), vmem((w, h), F32),
            vmem((n, n), F32), vmem((n, n), F32),
            vmem((m, wide), BF16), vmem((m, wide), BF16),
            vmem((n, m), BF16), vmem((n, m), BF16),
            vmem((n, wide), F32), vmem((nz, h, k), F32), vmem((nz, w, h), F32),
            vmem((nz, h, k), F32), vmem((nz, w, h), F32),
            gather_sems, list(gather_sems),
            *[dma((nz,)) for _ in range(8)],
            dma((8,)), dma((2, m // 256)),
        ],
        compiler_params=pltpu.CompilerParams(
            collective_id=0, has_side_effects=True, vmem_limit_bytes=VMEM_KIB * 1024
        ),
        name="panel_step",
    )(*(pltpu.with_memory_space_constraint(v, pltpu.HBM) for v in operands))
    return pa.T, to, ro, do.T


def solution(mesh):
    nz, ncol = mesh.shape["row"], mesh.shape["col"]
    side = math.isqrt(ncol // CORES)
    spec = P("row", "col")
    return jax.shard_map(
        functools.partial(on_device, nz, side),
        mesh=mesh,
        in_specs=(spec,) * 8,
        out_specs=(spec,) * 4,
        check_vma=False,
    )
```
